32 devices in a mesh: section: 4 (over z), tm: 8 (over y, x, core).
Axes of the slice: x: 2, y: 2, z: 4, core: 2. Of those that a mesh axis runs over, the one named last changes fastest.
Arguments:
- clean: float32 [4, 4, 512], P(None, None, 'tm'), may hold values from -6 to 6
- noise: float32 [4, 4, 512], P(None, None, 'tm'), may hold values from -6 to 6
- timestep: int32 [4], replicated, may hold values from 0 to 999
- lift: float32 [256], replicated, may hold values from -4 to 4
- norm_gain: float32 [4, 2, 256], P('section'), may hold values from 0.5 to 1.5
- norm_bias: float32 [4, 2, 256], P('section'), may hold values from -0.7 to 0.7
- conv_weight: bfloat16 [4, 2, 3, 3, 256, 256], P('section'), may hold values from -0.125 to 0.125
- time_proj: bfloat16 [4, 256, 256], P('section'), may hold values from -0.375 to 0.375
Outputs:
- skips: bfloat16 [4, 4, 4, 512, 256], P('section', None, None, 'tm')
The draws below stay inside these ranges and needn't reach their ends.
All inputs are finite; a program needn't handle non-finite values.
Results may differ from the reference program's by a relative error of at most 0.012.
Values may be sent and summed in bfloat16 or wider, within the bound.
A program may use at most 64 MiB of HBM per device.

```python
import math
import jax
import jax.numpy as jnp
from jax import lax

C = 256
GROUPS = 32
LAYERS = 2
MB = 4
FR = 4
STEPS = 1000
TD = 64
TIME = 512
N_SECTION = 4


def envelope(key):
    blocks = TIME // TD
    level_key, start_key = jax.random.split(jax.random.fold_in(key, 7001))
    log_level = jax.random.uniform(level_key, (MB, blocks), jnp.float32, -3.0, 1.5)
    run_length = min(3, blocks)
    run_start = jax.random.randint(start_key, (MB, 1), 0, blocks)
    positions = jnp.arange(blocks, dtype=jnp.int32)[None, :]
    silent = (positions - run_start) % blocks < run_length
    log_level = jnp.where(silent, -3.0, log_level)
    amplitude = jnp.exp(log_level)
    return jnp.repeat(amplitude, TD, axis=1)[:, None, :]


def draw_clean(key, part):
    amplitude = envelope(key)
    entry_key = jax.random.fold_in(key, 7002)
    entries = jax.random.normal(entry_key, (MB, FR, TIME), jnp.float32)
    return jnp.clip(entries * amplitude, -6.0, 6.0)


def draw_noise(key, part):
    amplitude = envelope(key)
    entry_key = jax.random.fold_in(key, 7003)
    entries = jax.random.normal(entry_key, (MB, FR, TIME), jnp.float32)
    return jnp.clip(entries * amplitude, -6.0, 6.0)


def touch_ends(drawn, stream_key, least, largest):
    spot = [jax.random.randint(jax.random.fold_in(stream_key, axis), (), 0, length) for axis, length in enumerate(drawn.shape)]
    main_axis = drawn.shape.index(max(drawn.shape))
    next_to = spot[:main_axis] + [(spot[main_axis] + 1) % drawn.shape[main_axis]] + spot[main_axis + 1:]
    return drawn.at[tuple(spot)].set(least).at[tuple(next_to)].set(largest)


def steps_of(rng, shape, shards, low, largest):
    factor_of = 1.0
    for dim, shards_of in shards:
        heights = jax.random.uniform(jax.random.fold_in(jax.random.fold_in(rng, 6), dim), (shards_of,), jnp.float32, low / len(shards), largest / len(shards))
        factor_of = factor_of * jnp.repeat(jnp.exp(heights), shape[dim] // shards_of).reshape((-1,) + (1,) * (len(shape) - 1 - dim))
    return factor_of


def normal_values(rng, extent, scale, bound, cuts=(), held_as=jnp.bfloat16):
    level = steps_of(rng, extent, cuts, -0.22, 0.18) if cuts else 1.0
    result = jax.random.normal(rng, extent, jnp.float32) * scale * level
    return jnp.minimum(jnp.maximum(result, -bound), bound).astype(held_as)


def setup_inputs(seed: int = 0) -> dict:
    splits = jax.random.split(jax.random.key(seed), 9)
    return {
        "clean": draw_clean(jax.random.fold_in(splits[8], 71), 0),
        "noise": draw_noise(jax.random.fold_in(splits[8], 71), 0),
        "timestep": touch_ends(jax.random.randint(splits[2], (MB,), 0, STEPS), jax.random.fold_in(splits[2], 1), 0, STEPS - 1).astype(jnp.int32),
        "lift": normal_values(splits[3], (C,), 1.0, 4.0, (), jnp.float32),
        "norm_gain": jnp.clip(1.0 + 0.1 * jax.random.normal(splits[4], (N_SECTION, LAYERS, C), jnp.float32), 0.5, 1.5),
        "norm_bias": jnp.clip(jax.random.uniform(splits[5], (N_SECTION, LAYERS, C), jnp.float32, -0.7, 0.7) * steps_of(splits[5], (N_SECTION, LAYERS, C), ((0, 4),), -0.4, 0.0), -0.7, 0.7),
        "conv_weight": normal_values(splits[6], (N_SECTION, LAYERS, 3, 3, C, C), (9 * C) ** -0.5, 0.125, ((0, 4),)),
        "time_proj": normal_values(splits[7], (N_SECTION, C, C), C ** -0.5, 0.375, ((0, 4),)),
    }


def prepare(clean, noise, timestep, lift):
    steps_f = timestep.astype(jnp.float32)
    level = jnp.cos(math.pi / 2.0 * (steps_f / STEPS + 0.008) / 1.008) ** 2
    noisy = jnp.sqrt(level)[:, None, None] * clean + jnp.sqrt(1.0 - level)[:, None, None] * noise
    lifted = (noisy[..., None] * lift).astype(jnp.bfloat16)
    half = C // 2
    freqs = jnp.exp(-math.log(10000.0) * jnp.arange(half, dtype=jnp.float32) / half)
    angles = steps_f[:, None] * freqs[None, :]
    emb = jnp.concatenate([jnp.sin(angles), jnp.cos(angles)], axis=1).astype(jnp.bfloat16)
    return (lifted, emb)

def group_act(h, gain, bias):
    rows_f, rows_t, width = h.shape
    grouped = h.reshape(rows_f, rows_t, GROUPS, width // GROUPS)
    count = rows_f * rows_t * (width // GROUPS)
    total = lax.optimization_barrier(jnp.sum(grouped, axis=(0, 1, 3)))
    square = lax.optimization_barrier(jnp.sum(grouped * grouped, axis=(0, 1, 3)))
    mean = total / count
    var = square / count - mean * mean
    inv = lax.rsqrt(var + 1e-05)
    normed = ((grouped - mean[:, None]) * inv[:, None]).reshape(h.shape) * gain + bias
    return jax.nn.silu(normed).astype(jnp.bfloat16)

def conv_same(padded, weight):
    rows_f = padded.shape[0]
    width_out = padded.shape[1] - 2
    chans = padded.shape[2]
    framed = jnp.pad(padded, ((1, 1), (0, 0), (0, 0)))
    total = jnp.zeros((rows_f * width_out, weight.shape[3]), jnp.float32)
    for i in range(3):
        for j in range(3):
            window = framed[i:i + rows_f, j:j + width_out].reshape(-1, chans)
            total = total + jnp.dot(window, weight[i, j], preferred_element_type=jnp.float32)
    return total.reshape(rows_f, width_out, weight.shape[3])

def reference(clean, noise, timestep, lift, norm_gain, norm_bias, conv_weight, time_proj):
    lifted, emb = prepare(clean, noise, timestep, lift)
    levels = []
    for section_id in range(N_SECTION):
        levels.append(jnp.dot(emb, time_proj[section_id], preferred_element_type=jnp.float32))
    results = []
    for micro in range(MB):
        current = lifted[micro]
        per_level = []
        for section_id in range(N_SECTION):
            depth = LAYERS if section_id < N_SECTION // 2 else 1
            hidden = current.astype(jnp.float32) + levels[section_id][micro]
            for layer in range(depth):
                act = group_act(hidden, norm_gain[section_id, layer], norm_bias[section_id, layer])
                padded = jnp.pad(act, ((0, 0), (1, 1), (0, 0)))
                hidden = hidden + conv_same(padded, conv_weight[section_id, layer])
            current = hidden.astype(jnp.bfloat16)
            per_level.append(current)
        results.append(jnp.stack(per_level))
    return jnp.stack(results, axis=1)
```

```python
import functools
import math

import jax
import jax.numpy as jnp
from jax import lax
from jax.experimental import pallas as pl
from jax.experimental.pallas import tpu as pltpu
from jax.sharding import PartitionSpec as P

GROUPS = 32
STEPS = 1000
MESH = pl.DeviceIdType.MESH


def prepare(clean, noise, timestep, lift):
    chans = lift.shape[0]
    steps_f = timestep.astype(jnp.float32)
    level = jnp.cos(math.pi / 2.0 * (steps_f / STEPS + 0.008) / 1.008) ** 2
    noisy = jnp.sqrt(level)[:, None, None] * clean + jnp.sqrt(1.0 - level)[:, None, None] * noise
    lifted = (noisy[..., None] * lift).astype(jnp.bfloat16)
    half = chans // 2
    freqs = jnp.exp(-math.log(10000.0) * jnp.arange(half, dtype=jnp.float32) / half)
    angles = steps_f[:, None] * freqs[None, :]
    emb = jnp.concatenate([jnp.sin(angles), jnp.cos(angles)], axis=1).astype(jnp.bfloat16)
    return (lifted, emb)


def silu(z):
    half = 0.5 * z
    return half + half * jnp.tanh(half)


def kernel(
    dims,
    lifted,
    temb,
    gains,
    biases,
    weights,
    out,
    w,
    xin,
    hmid,
    staged,
    act3,
    st_send,
    st_recv,
    edge_send,
    edge_recv,
    st_ssem,
    st_rsem,
    edge_ssem,
    edge_rsem,
    blk_ssem,
    blk_rsem,
    w_sem,
    out_sem,
):
    n_time, n_section, micros, rows_f, frames, chans, layers = dims
    rows = rows_f * frames
    positions = rows * n_time
    width = chans // GROUPS
    count = positions * width
    sec = lax.axis_index("section")
    tm = lax.axis_index("tm")
    deep = sec < n_section // 2
    first = sec == 0
    last = sec == n_section - 1
    has_left = tm > 0
    has_right = tm < n_time - 1
    up = jnp.minimum(sec + 1, n_section - 1)
    down = jnp.maximum(sec - 1, 0)
    short = n_time <= 8

    def load_w(layer):
        return pltpu.make_async_copy(weights.at[layer], w.at[layer], w_sem.at[layer])

    load_w(0).start()

    @pl.when(deep)
    def _():
        for layer in range(1, layers):
            load_w(layer).start()

    barrier = pltpu.get_barrier_semaphore()

    def peers(section, begin):
        def one(r, carry):
            pl.semaphore_signal(
                barrier,
                inc=1,
                device_id=(section, lax.rem(tm + r, n_time)),
                device_id_type=MESH,
            )
            return carry

        lax.fori_loop(begin, n_time, one, 0, unroll=short)

    peers(sec, 1)

    @pl.when(jnp.logical_not(last))
    def _():
        peers(up, 0)

    @pl.when(jnp.logical_not(first))
    def _():
        peers(down, 0)

    def x_load(m):
        return pltpu.make_async_copy(lifted.at[m], xin.at[m], blk_rsem.at[m])

    @pl.when(first)
    def _():
        for m in range(micros):
            x_load(m).start()

    act3[0:frames, :] = jnp.zeros((frames, 3 * chans), jnp.bfloat16)
    act3[rows + frames : rows + 2 * frames, :] = jnp.zeros((frames, 3 * chans), jnp.bfloat16)

    def summarize(m, kind, value):
        st_send[m, kind, :, 0:chans] = jnp.sum(value, axis=0, keepdims=True)
        st_send[m, kind, :, chans : 2 * chans] = jnp.sum(value * value, axis=0, keepdims=True)
        for f in range(rows_f):
            edge_send[m, kind, 0, f : f + 1, :] = value[f * frames : f * frames + 1]
            edge_send[m, kind, 1, f : f + 1, :] = value[(f + 1) * frames - 1 : (f + 1) * frames]

    def edge_copy(m, kind, slot, side, section, peer):
        return pltpu.make_async_remote_copy(
            src_ref=edge_send.at[m, kind, side],
            dst_ref=edge_recv.at[m, slot, 1 - side],
            send_sem=edge_ssem.at[m, kind, side],
            recv_sem=edge_rsem.at[m, slot, 1 - side],
            device_id=(section, peer),
            device_id_type=MESH,
        )

    def publish(m, kind, slot, section, begin):
        def one(r, carry):
            pltpu.make_async_remote_copy(
                src_ref=st_send.at[m, kind],
                dst_ref=st_recv.at[m, slot, tm],
                send_sem=st_ssem.at[m, kind],
                recv_sem=st_rsem.at[m, slot],
                device_id=(section, lax.rem(tm + r, n_time)),
                device_id_type=MESH,
            ).start()
            return carry

        lax.fori_loop(begin, n_time, one, 0, unroll=short)
        if begin:
            st_recv[m, slot, tm] = st_send[m, kind]

        @pl.when(has_left)
        def _():
            edge_copy(m, kind, slot, 0, section, jnp.maximum(tm - 1, 0)).start()

        @pl.when(has_right)
        def _():
            edge_copy(m, kind, slot, 1, section, jnp.minimum(tm + 1, n_time - 1)).start()

    def drain(m, kind, begin):
        whole = st_recv.at[m, 0, pl.ds(0, n_time - begin)]
        pltpu.make_async_copy(whole, whole, st_ssem.at[m, kind]).wait()

        @pl.when(has_left)
        def _():
            pltpu.make_async_copy(
                edge_send.at[m, kind, 0], edge_send.at[m, kind, 0], edge_ssem.at[m, kind, 0]
            ).wait()

        @pl.when(has_right)
        def _():
            pltpu.make_async_copy(
                edge_send.at[m, kind, 1], edge_send.at[m, kind, 1], edge_ssem.at[m, kind, 1]
            ).wait()

    def await_stats(m, slot, begin):
        whole = st_recv.at[m, slot, pl.ds(0, n_time - begin)]
        pltpu.make_async_copy(whole, whole, st_rsem.at[m, slot]).wait()

    def await_edges(m, slot):
        @pl.when(has_left)
        def _():
            pltpu.make_async_copy(
                edge_recv.at[m, slot, 0], edge_recv.at[m, slot, 0], edge_rsem.at[m, slot, 0]
            ).wait()

        @pl.when(has_right)
        def _():
            pltpu.make_async_copy(
                edge_recv.at[m, slot, 1], edge_recv.at[m, slot, 1], edge_rsem.at[m, slot, 1]
            ).wait()

    lanes = lax.broadcasted_iota(jnp.int32, (8, 2 * chans), 1)

    def group_total(pair):
        total = jnp.broadcast_to(pair, (8, 2 * chans))
        step = 1
        while step < width:
            ahead = pltpu.roll(total, 2 * chans - step, 1)
            behind = pltpu.roll(total, step, 1)
            total = total + jnp.where((lanes // step) % 2 == 0, ahead, behind)
            step *= 2
        return total[0:1]

    def convolve(m, slot, layer, hidden, shift_row):
        stats = jnp.sum(st_recv[m, slot], axis=0)
        s1 = stats[:, 0:chans]
        s2 = stats[:, chans : 2 * chans]
        if shift_row is not None:
            s2 = s2 + 2.0 * shift_row * s1 + positions * (shift_row * shift_row)
            s1 = s1 + positions * shift_row
        total = group_total(jnp.concatenate([s1, s2], axis=1))
        mean = total[:, 0:chans] / count
        var = total[:, chans : 2 * chans] / count - mean * mean
        scale = lax.rsqrt(var + 1e-05) * gains[layer]
        offset = biases[layer] - mean * scale
        act = silu(hidden * scale + offset)
        edges = edge_recv[m, slot]
        if shift_row is not None:
            edges = edges + shift_row
        edges = silu(edges * scale + offset)
        before = jnp.where(has_left, edges[0], 0.0)
        after = jnp.where(has_right, edges[1], 0.0)
        place = lax.broadcasted_iota(jnp.int32, (frames, chans), 0)
        for f in range(rows_f):
            part = act[f * frames : (f + 1) * frames]
            prev = jnp.where(place == 0, before[f : f + 1], pltpu.roll(part, 1, 0))
            nxt = jnp.where(place == frames - 1, after[f : f + 1], pltpu.roll(part, frames - 1, 0))
            at = slice((f + 1) * frames, (f + 2) * frames)
            act3[at, 0:chans] = prev.astype(jnp.bfloat16)
            act3[at, chans : 2 * chans] = part.astype(jnp.bfloat16)
            act3[at, 2 * chans : 3 * chans] = nxt.astype(jnp.bfloat16)
        total = hidden
        for i in range(3):
            total = total + jnp.dot(
                act3[i * frames : i * frames + rows],
                w[layer, i],
                preferred_element_type=jnp.float32,
            )
        return total

    def block_copy(m):
        return pltpu.make_async_remote_copy(
            src_ref=staged.at[m],
            dst_ref=xin.at[m],
            send_sem=blk_ssem.at[m],
            recv_sem=blk_rsem.at[m],
            device_id=(up, tm),
            device_id_type=MESH,
        )

    def out_copy(m):
        return pltpu.make_async_copy(staged.at[m], out.at[m], out_sem.at[m])

    def finish(m, hidden):
        rounded = hidden.astype(jnp.bfloat16)
        staged[m] = rounded

        @pl.when(jnp.logical_not(last))
        def _():
            summarize(m, 2, rounded.astype(jnp.float32))
            publish(m, 2, 0, up, 0)
            block_copy(m).start()

        out_copy(m).start()

    def enter(m):
        @pl.when(first)
        def _():
            await_stats(m, 0, 1)

        @pl.when(jnp.logical_not(first))
        def _():
            await_stats(m, 0, 0)
            pltpu.make_async_copy(xin.at[m], xin.at[m], blk_rsem.at[m]).wait()

        await_edges(m, 0)
        shift_row = temb[m]
        hidden = xin[m].astype(jnp.float32) + shift_row
        hidden = convolve(m, 0, 0, hidden, shift_row)

        @pl.when(deep)
        def _():
            hmid[m] = hidden
            summarize(m, 1, hidden)
            publish(m, 1, 1, sec, 1)

        @pl.when(jnp.logical_not(deep))
        def _():
            finish(m, hidden)

    def leave(m):
        @pl.when(deep)
        def _():
            await_stats(m, 1, 1)
            await_edges(m, 1)
            finish(m, convolve(m, 1, 1, hmid[m], None))

    @pl.when(first)
    def _():
        for m in range(micros):
            x_load(m).wait()
            summarize(m, 0, xin[m].astype(jnp.float32))

    arrivals = n_time - 1
    arrivals = arrivals + n_time * jnp.where(last, 0, 1) + n_time * jnp.where(first, 0, 1)
    pl.semaphore_wait(barrier, arrivals)

    @pl.when(first)
    def _():
        for m in range(micros):
            publish(m, 0, 0, sec, 1)

    load_w(0).wait()

    @pl.when(deep)
    def _():
        for layer in range(1, layers):
            load_w(layer).wait()

    enter(0)
    for m in range(1, micros):
        enter(m)
        leave(m - 1)
    leave(micros - 1)

    @pl.when(first)
    def _():
        for m in range(micros):
            drain(m, 0, 1)

    @pl.when(deep)
    def _():
        for m in range(micros):
            drain(m, 1, 1)

    @pl.when(jnp.logical_not(last))
    def _():
        for m in range(micros):
            drain(m, 2, 0)
            block_copy(m).wait_send()

    for m in range(micros):
        out_copy(m).wait()


def on_device(clean, noise, timestep, lift, norm_gain, norm_bias, conv_weight, time_proj):
    lifted, emb = prepare(clean, noise, timestep, lift)
    temb = jnp.dot(emb, time_proj[0], preferred_element_type=jnp.float32)
    n_time = lax.axis_size("tm")
    n_section = lax.axis_size("section")
    micros, rows_f, frames, chans = lifted.shape
    layers = norm_gain.shape[1]
    rows = rows_f * frames
    dims = (n_time, n_section, micros, rows_f, frames, chans, layers)
    vmem = pl.BlockSpec(memory_space=pltpu.VMEM)
    hbm = pl.BlockSpec(memory_space=pl.ANY)
    dma = pltpu.SemaphoreType.DMA
    saved = pl.pallas_call(
        functools.partial(kernel, dims),
        out_shape=jax.ShapeDtypeStruct((micros, rows, chans), jnp.bfloat16),
        in_specs=[hbm, vmem, vmem, vmem, hbm],
        out_specs=hbm,
        scratch_shapes=[
            pltpu.VMEM((layers, 3, 3 * chans, chans), jnp.bfloat16),
            pltpu.VMEM((micros, rows, chans), jnp.bfloat16),
            pltpu.VMEM((micros, rows, chans), jnp.float32),
            pltpu.VMEM((micros, rows, chans), jnp.bfloat16),
            pltpu.VMEM((rows + 2 * frames, 3 * chans), jnp.bfloat16),
            pltpu.VMEM((micros, 3, 1, 2 * chans), jnp.float32),
            pltpu.VMEM((micros, 2, n_time, 1, 2 * chans), jnp.float32),
            pltpu.VMEM((micros, 3, 2, rows_f, chans), jnp.float32),
            pltpu.VMEM((micros, 2, 2, rows_f, chans), jnp.float32),
            dma((micros, 3)),
            dma((micros, 2)),
            dma((micros, 3, 2)),
            dma((micros, 2, 2)),
            dma((micros,)),
            dma((micros,)),
            dma((layers,)),
            dma((micros,)),
        ],
        compiler_params=pltpu.CompilerParams(collective_id=0, has_side_effects=True),
    )(
        lifted.reshape(micros, rows, chans),
        temb.reshape(micros, 1, chans),
        norm_gain.reshape(layers, 1, chans),
        norm_bias.reshape(layers, 1, chans),
        conv_weight.reshape(layers, 3, 3 * chans, chans),
    )
    return saved.reshape(1, micros, rows_f, frames, chans)


def solution(mesh):
    in_specs = (
        P(None, None, "tm"),
        P(None, None, "tm"),
        P(),
        P(),
        P("section", None, None),
        P("section", None, None),
        P("section", None, None, None, None, None),
        P("section", None, None),
    )
    out_specs = P("section", None, None, "tm", None)
    return jax.shard_map(
        on_device, mesh=mesh, in_specs=in_specs, out_specs=out_specs, check_vma=False
    )
```

```python
import functools
import math

import jax
import jax.numpy as jnp
from jax import lax
from jax.experimental import pallas as pl
from jax.experimental.pallas import tpu as pltpu
from jax.sharding import PartitionSpec as P

GROUPS = 32
STEPS = 1000
MESH = pl.DeviceIdType.MESH


def silu(z):
    half = 0.5 * z
    return half + half * jnp.tanh(half)


def kernel(
    dims,
    timestep,
    clean_in,
    noise_in,
    lift_in,
    gains_in,
    biases_in,
    proj_in,
    weights,
    staged,
    w,
    xin,
    hmid,
    clean,
    noise,
    lift,
    gains,
    biases,
    proj,
    noisy,
    temb,
    act3,
    st_send,
    st_recv,
    edge_send,
    edge_recv,
    st_ssem,
    st_rsem,
    edge_ssem,
    edge_rsem,
    blk_ssem,
    blk_rsem,
    w_sem,
    in_sem,
):
    n_time, n_section, micros, rows_f, frames, chans, layers = dims
    rows = rows_f * frames
    positions = rows * n_time
    width = chans // GROUPS
    count = positions * width
    sec = lax.axis_index("section")
    tm = lax.axis_index("tm")
    deep = sec < n_section // 2
    first = sec == 0
    last = sec == n_section - 1
    has_left = tm > 0
    has_right = tm < n_time - 1
    up = jnp.minimum(sec + 1, n_section - 1)
    down = jnp.maximum(sec - 1, 0)
    short = n_time <= 8

    def load_w(layer):
        return pltpu.make_async_copy(weights.at[layer], w.at[layer], w_sem.at[layer])

    small = [
        pltpu.make_async_copy(src, dst, in_sem.at[k])
        for k, (src, dst) in enumerate(
            [
                (proj_in.at[0], proj),
                (gains_in.at[0], gains),
                (biases_in.at[0], biases),
                (clean_in, clean),
                (noise_in, noise),
                (lift_in, lift),
            ]
        )
    ]
    for copy in small[:3]:
        copy.start()

    @pl.when(first)
    def _():
        for copy in small[3:]:
            copy.start()

    barrier = pltpu.get_barrier_semaphore()

    def peers(section, begin):
        def one(r, carry):
            pl.semaphore_signal(
                barrier,
                inc=1,
                device_id=(section, lax.rem(tm + r, n_time)),
                device_id_type=MESH,
            )
            return carry

        lax.fori_loop(begin, n_time, one, 0, unroll=short)

    peers(sec, 1)

    @pl.when(jnp.logical_not(last))
    def _():
        peers(up, 0)

    @pl.when(jnp.logical_not(first))
    def _():
        peers(down, 0)

    load_w(0).start()

    @pl.when(deep)
    def _():
        for layer in range(1, layers):
            load_w(layer).start()

    act3[0:frames, :] = jnp.zeros((frames, 3 * chans), jnp.bfloat16)
    act3[rows + frames : rows + 2 * frames, :] = jnp.zeros((frames, 3 * chans), jnp.bfloat16)

    def summarize(m, kind, value):
        st_send[m, kind, :, 0:chans] = jnp.sum(value, axis=0, keepdims=True)
        st_send[m, kind, :, chans : 2 * chans] = jnp.sum(value * value, axis=0, keepdims=True)
        for f in range(rows_f):
            edge_send[m, kind, 0, f : f + 1, :] = value[f * frames : f * frames + 1]
            edge_send[m, kind, 1, f : f + 1, :] = value[(f + 1) * frames - 1 : (f + 1) * frames]

    def edge_copy(m, kind, slot, side, section, peer):
        return pltpu.make_async_remote_copy(
            src_ref=edge_send.at[m, kind, side],
            dst_ref=edge_recv.at[m, slot, 1 - side],
            send_sem=edge_ssem.at[m, kind, side],
            recv_sem=edge_rsem.at[m, slot, 1 - side],
            device_id=(section, peer),
            device_id_type=MESH,
        )

    def publish(m, kind, slot, section, begin):
        def one(r, carry):
            pltpu.make_async_remote_copy(
                src_ref=st_send.at[m, kind],
                dst_ref=st_recv.at[m, slot, tm],
                send_sem=st_ssem.at[m, kind],
                recv_sem=st_rsem.at[m, slot],
                device_id=(section, lax.rem(tm + r, n_time)),
                device_id_type=MESH,
            ).start()
            return carry

        lax.fori_loop(begin, n_time, one, 0, unroll=short)
        if begin:
            st_recv[m, slot, tm] = st_send[m, kind]

        @pl.when(has_left)
        def _():
            edge_copy(m, kind, slot, 0, section, jnp.maximum(tm - 1, 0)).start()

        @pl.when(has_right)
        def _():
            edge_copy(m, kind, slot, 1, section, jnp.minimum(tm + 1, n_time - 1)).start()

    def drain(m, kind, begin):
        whole = st_recv.at[m, 0, pl.ds(0, n_time - begin)]
        pltpu.make_async_copy(whole, whole, st_ssem.at[m, kind]).wait()

        @pl.when(has_left)
        def _():
            pltpu.make_async_copy(
                edge_send.at[m, kind, 0], edge_send.at[m, kind, 0], edge_ssem.at[m, kind, 0]
            ).wait()

        @pl.when(has_right)
        def _():
            pltpu.make_async_copy(
                edge_send.at[m, kind, 1], edge_send.at[m, kind, 1], edge_ssem.at[m, kind, 1]
            ).wait()

    def await_stats(m, slot, begin):
        whole = st_recv.at[m, slot, pl.ds(0, n_time - begin)]
        pltpu.make_async_copy(whole, whole, st_rsem.at[m, slot]).wait()

    def await_edges(m, slot):
        @pl.when(has_left)
        def _():
            pltpu.make_async_copy(
                edge_recv.at[m, slot, 0], edge_recv.at[m, slot, 0], edge_rsem.at[m, slot, 0]
            ).wait()

        @pl.when(has_right)
        def _():
            pltpu.make_async_copy(
                edge_recv.at[m, slot, 1], edge_recv.at[m, slot, 1], edge_rsem.at[m, slot, 1]
            ).wait()

    lanes = lax.broadcasted_iota(jnp.int32, (8, 2 * chans), 1)

    def group_total(pair):
        total = jnp.broadcast_to(pair, (8, 2 * chans))
        step = 1
        while step < width:
            ahead = pltpu.roll(total, 2 * chans - step, 1)
            behind = pltpu.roll(total, step, 1)
            total = total + jnp.where((lanes // step) % 2 == 0, ahead, behind)
            step *= 2
        return total[0:1]

    def convolve(m, slot, layer, hidden, shift_row):
        stats = jnp.sum(st_recv[m, slot], axis=0)
        s1 = stats[:, 0:chans]
        s2 = stats[:, chans : 2 * chans]
        if shift_row is not None:
            s2 = s2 + 2.0 * shift_row * s1 + positions * (shift_row * shift_row)
            s1 = s1 + positions * shift_row
        total = group_total(jnp.concatenate([s1, s2], axis=1))
        mean = total[:, 0:chans] / count
        var = total[:, chans : 2 * chans] / count - mean * mean
        scale = lax.rsqrt(var + 1e-05) * gains[layer : layer + 1, :]
        offset = biases[layer : layer + 1, :] - mean * scale
        act = silu(hidden * scale + offset)
        edges = edge_recv[m, slot]
        if shift_row is not None:
            edges = edges + shift_row
        edges = silu(edges * scale + offset)
        before = jnp.where(has_left, edges[0], 0.0)
        after = jnp.where(has_right, edges[1], 0.0)
        place = lax.broadcasted_iota(jnp.int32, (frames, chans), 0)
        for f in range(rows_f):
            part = act[f * frames : (f + 1) * frames]
            prev = jnp.where(place == 0, before[f : f + 1], pltpu.roll(part, 1, 0))
            nxt = jnp.where(place == frames - 1, after[f : f + 1], pltpu.roll(part, frames - 1, 0))
            at = slice((f + 1) * frames, (f + 2) * frames)
            act3[at, 0:chans] = prev.astype(jnp.bfloat16)
            act3[at, chans : 2 * chans] = part.astype(jnp.bfloat16)
            act3[at, 2 * chans : 3 * chans] = nxt.astype(jnp.bfloat16)
        total = hidden
        for i in range(3):
            total = total + jnp.dot(
                act3[i * frames : i * frames + rows],
                w[layer, i],
                preferred_element_type=jnp.float32,
            )
        return total

    def block_copy(m):
        return pltpu.make_async_remote_copy(
            src_ref=staged.at[m],
            dst_ref=xin.at[m],
            send_sem=blk_ssem.at[m],
            recv_sem=blk_rsem.at[m],
            device_id=(up, tm),
            device_id_type=MESH,
        )

    def finish(m, hidden):
        rounded = hidden.astype(jnp.bfloat16)
        staged[m] = rounded

        @pl.when(jnp.logical_not(last))
        def _():
            summarize(m, 2, rounded.astype(jnp.float32))
            publish(m, 2, 0, up, 0)
            block_copy(m).start()

    def enter(m):
        @pl.when(first)
        def _():
            await_stats(m, 0, 1)

        @pl.when(jnp.logical_not(first))
        def _():
            await_stats(m, 0, 0)
            pltpu.make_async_copy(xin.at[m], xin.at[m], blk_rsem.at[m]).wait()

        await_edges(m, 0)
        shift_row = temb[m : m + 1, :]
        hidden = xin[m].astype(jnp.float32) + shift_row
        hidden = convolve(m, 0, 0, hidden, shift_row)

        @pl.when(deep)
        def _():
            hmid[m] = hidden
            summarize(m, 1, hidden)
            publish(m, 1, 1, sec, 1)

        @pl.when(jnp.logical_not(deep))
        def _():
            finish(m, hidden)

    def leave(m):
        @pl.when(deep)
        def _():
            await_stats(m, 1, 1)
            await_edges(m, 1)
            finish(m, convolve(m, 1, 1, hmid[m], None))

    half = chans // 2
    slots = temb.shape[0]
    which = lax.broadcasted_iota(jnp.int32, (slots, half), 0)
    steps_f = jnp.zeros((slots, half), jnp.float32)
    for m in range(micros):
        steps_f = jnp.where(which == m, timestep[m].astype(jnp.float32), steps_f)

    @pl.when(first)
    def _():
        level = jnp.cos(math.pi / 2.0 * (steps_f / STEPS + 0.008) / 1.008) ** 2
        keep = jnp.sqrt(level)
        blur = jnp.sqrt(1.0 - level)
        for copy in small[3:]:
            copy.wait()
        for m in range(micros):
            noisy[m * rows_f : (m + 1) * rows_f, :] = (
                keep[m : m + 1, 0:1] * clean[m] + blur[m : m + 1, 0:1] * noise[m]
            )
        columns = jnp.transpose(noisy[...])
        for m in range(micros):
            for f in range(rows_f):
                at = m * rows_f + f
                xin[m, f * frames : (f + 1) * frames, :] = (
                    columns[:, at : at + 1] * lift[...]
                ).astype(jnp.bfloat16)
            summarize(m, 0, xin[m].astype(jnp.float32))

    order = lax.broadcasted_iota(jnp.int32, (slots, half), 1).astype(jnp.float32)
    angles = steps_f * jnp.exp(-math.log(10000.0) * order / half)
    for copy in small[:3]:
        copy.wait()
    temb[...] = jnp.dot(
        jnp.sin(angles).astype(jnp.bfloat16), proj[0:half, :], preferred_element_type=jnp.float32
    ) + jnp.dot(
        jnp.cos(angles).astype(jnp.bfloat16), proj[half:chans, :], preferred_element_type=jnp.float32
    )

    arrivals = n_time - 1
    arrivals = arrivals + n_time * jnp.where(last, 0, 1) + n_time * jnp.where(first, 0, 1)
    pl.semaphore_wait(barrier, arrivals)

    @pl.when(first)
    def _():
        for m in range(micros):
            publish(m, 0, 0, sec, 1)

    load_w(0).wait()

    @pl.when(deep)
    def _():
        for layer in range(1, layers):
            load_w(layer).wait()

    enter(0)
    for m in range(1, micros):
        enter(m)
        leave(m - 1)
    leave(micros - 1)

    @pl.when(first)
    def _():
        for m in range(micros):
            drain(m, 0, 1)

    @pl.when(deep)
    def _():
        for m in range(micros):
            drain(m, 1, 1)

    @pl.when(jnp.logical_not(last))
    def _():
        for m in range(micros):
            drain(m, 2, 0)
            block_copy(m).wait_send()


def on_device(clean, noise, timestep, lift, norm_gain, norm_bias, conv_weight, time_proj):
    n_time = lax.axis_size("tm")
    n_section = lax.axis_size("section")
    micros, rows_f, frames = clean.shape
    chans = lift.shape[0]
    layers = norm_gain.shape[1]
    slots = -(-micros // 8) * 8
    rows = rows_f * frames
    dims = (n_time, n_section, micros, rows_f, frames, chans, layers)
    vmem = pl.BlockSpec(memory_space=pltpu.VMEM)
    hbm = pl.BlockSpec(memory_space=pl.ANY)
    dma = pltpu.SemaphoreType.DMA
    saved = pl.pallas_call(
        functools.partial(kernel, dims),
        out_shape=jax.ShapeDtypeStruct((micros, rows, chans), jnp.bfloat16),
        in_specs=[pl.BlockSpec(memory_space=pltpu.SMEM)] + [hbm] * 7,
        out_specs=vmem,
        scratch_shapes=[
            pltpu.VMEM((layers, 3, 3 * chans, chans), jnp.bfloat16),
            pltpu.VMEM((micros, rows, chans), jnp.bfloat16),
            pltpu.VMEM((micros, rows, chans), jnp.float32),
            pltpu.VMEM((micros, rows_f, frames), jnp.float32),
            pltpu.VMEM((micros, rows_f, frames), jnp.float32),
            pltpu.VMEM((1, chans), jnp.float32),
            pltpu.VMEM((layers, chans), jnp.float32),
            pltpu.VMEM((layers, chans), jnp.float32),
            pltpu.VMEM((chans, chans), jnp.bfloat16),
            pltpu.VMEM((micros * rows_f, frames), jnp.float32),
            pltpu.VMEM((slots, chans), jnp.float32),
            pltpu.VMEM((rows + 2 * frames, 3 * chans), jnp.bfloat16),
            pltpu.VMEM((micros, 3, 1, 2 * chans), jnp.float32),
            pltpu.VMEM((micros, 2, n_time, 1, 2 * chans), jnp.float32),
            pltpu.VMEM((micros, 3, 2, rows_f, chans), jnp.float32),
            pltpu.VMEM((micros, 2, 2, rows_f, chans), jnp.float32),
            dma((micros, 3)),
            dma((micros, 2)),
            dma((micros, 3, 2)),
            dma((micros, 2, 2)),
            dma((micros,)),
            dma((micros,)),
            dma((layers,)),
            dma((6,)),
        ],
        compiler_params=pltpu.CompilerParams(
            collective_id=0, has_side_effects=True
        ),
    )(
        timestep,
        clean,
        noise,
        lift.reshape(1, chans),
        norm_gain,
        norm_bias,
        time_proj,
        conv_weight.reshape(layers, 3, 3 * chans, chans),
    )
    return saved.reshape(1, micros, rows_f, frames, chans)


def solution(mesh):
    in_specs = (
        P(None, None, "tm"),
        P(None, None, "tm"),
        P(),
        P(),
        P("section", None, None),
        P("section", None, None),
        P("section", None, None, None, None, None),
        P("section", None, None),
    )
    out_specs = P("section", None, None, "tm", None)
    return jax.shard_map(
        on_device, mesh=mesh, in_specs=in_specs, out_specs=out_specs, check_vma=False
    )
```

```python
import functools
import math

import jax
import jax.numpy as jnp
from jax import lax
from jax.experimental import pallas as pl
from jax.experimental.pallas import tpu as pltpu
from jax.sharding import PartitionSpec as P

GROUPS = 32
STEPS = 1000
MESH = pl.DeviceIdType.MESH


def silu(z):
    half = 0.5 * z
    return half + half * jnp.tanh(half)


def kernel(
    dims,
    steps_in,
    clean_in,
    noise_in,
    lift_in,
    gains_in,
    biases_in,
    proj_in,
    weights,
    staged,
    w,
    xin,
    hmid,
    clean,
    noise,
    lift,
    gains,
    biases,
    proj,
    noisy,
    temb,
    timestep,
    act3,
    st_send,
    st_recv,
    edge_send,
    edge_recv,
    st_ssem,
    st_rsem,
    edge_ssem,
    edge_rsem,
    blk_ssem,
    blk_rsem,
    w_sem,
    in_sem,
):
    n_time, n_section, micros, rows_f, frames, chans, layers = dims
    rows = rows_f * frames
    positions = rows * n_time
    width = chans // GROUPS
    count = positions * width
    sec = lax.axis_index("section")
    tm = lax.axis_index("tm")
    deep = sec < n_section // 2
    first = sec == 0
    last = sec == n_section - 1
    has_left = tm > 0
    has_right = tm < n_time - 1
    up = jnp.minimum(sec + 1, n_section - 1)
    down = jnp.maximum(sec - 1, 0)
    short = n_time <= 8

    def load_w(layer):
        return pltpu.make_async_copy(weights.at[layer], w.at[layer], w_sem.at[layer])

    small = [
        pltpu.make_async_copy(src, dst, in_sem.at[k])
        for k, (src, dst) in enumerate(
            [
                (steps_in, timestep),
                (proj_in.at[0], proj),
                (gains_in.at[0], gains),
                (biases_in.at[0], biases),
                (clean_in, clean),
                (noise_in, noise),
                (lift_in, lift),
            ]
        )
    ]
    for copy in small[:4]:
        copy.start()

    @pl.when(first)
    def _():
        for copy in small[4:]:
            copy.start()

    barrier = pltpu.get_barrier_semaphore()

    def peers(section, begin):
        def one(r, carry):
            pl.semaphore_signal(
                barrier,
                inc=1,
                device_id=(section, lax.rem(tm + r, n_time)),
                device_id_type=MESH,
            )
            return carry

        lax.fori_loop(begin, n_time, one, 0, unroll=short)

    @pl.when(jnp.logical_not(first))
    def _():
        peers(down, 0)

    peers(sec, 1)

    load_w(0).start()

    @pl.when(deep)
    def _():
        for layer in range(1, layers):
            load_w(layer).start()

    def summarize(m, kind, value):
        st_send[m, kind, :, 0:chans] = jnp.sum(value, axis=0, keepdims=True)
        st_send[m, kind, :, chans : 2 * chans] = jnp.sum(value * value, axis=0, keepdims=True)
        for f in range(rows_f):
            edge_send[m, kind, 0, f : f + 1, :] = value[f * frames : f * frames + 1]
            edge_send[m, kind, 1, f : f + 1, :] = value[(f + 1) * frames - 1 : (f + 1) * frames]

    def edge_copy(m, kind, slot, side, section, peer):
        return pltpu.make_async_remote_copy(
            src_ref=edge_send.at[m, kind, side],
            dst_ref=edge_recv.at[m, slot, 1 - side],
            send_sem=edge_ssem.at[m, kind, side],
            recv_sem=edge_rsem.at[m, slot, 1 - side],
            device_id=(section, peer),
            device_id_type=MESH,
        )

    def publish(m, kind, slot, section, begin):
        def one(r, carry):
            pltpu.make_async_remote_copy(
                src_ref=st_send.at[m, kind],
                dst_ref=st_recv.at[m, slot, tm],
                send_sem=st_ssem.at[m, kind],
                recv_sem=st_rsem.at[m, slot],
                device_id=(section, lax.rem(tm + r, n_time)),
                device_id_type=MESH,
            ).start()
            return carry

        lax.fori_loop(begin, n_time, one, 0, unroll=short)
        if begin:
            st_recv[m, slot, tm] = st_send[m, kind]

        @pl.when(has_left)
        def _():
            edge_copy(m, kind, slot, 0, section, jnp.maximum(tm - 1, 0)).start()

        @pl.when(has_right)
        def _():
            edge_copy(m, kind, slot, 1, section, jnp.minimum(tm + 1, n_time - 1)).start()

    def drain(m, kind, begin):
        whole = st_recv.at[m, 0, pl.ds(0, n_time - begin)]
        pltpu.make_async_copy(whole, whole, st_ssem.at[m, kind]).wait()

        @pl.when(has_left)
        def _():
            pltpu.make_async_copy(
                edge_send.at[m, kind, 0], edge_send.at[m, kind, 0], edge_ssem.at[m, kind, 0]
            ).wait()

        @pl.when(has_right)
        def _():
            pltpu.make_async_copy(
                edge_send.at[m, kind, 1], edge_send.at[m, kind, 1], edge_ssem.at[m, kind, 1]
            ).wait()

    def await_stats(m, slot, begin):
        whole = st_recv.at[m, slot, pl.ds(0, n_time - begin)]
        pltpu.make_async_copy(whole, whole, st_rsem.at[m, slot]).wait()

    def await_edges(m, slot):
        @pl.when(has_left)
        def _():
            pltpu.make_async_copy(
                edge_recv.at[m, slot, 0], edge_recv.at[m, slot, 0], edge_rsem.at[m, slot, 0]
            ).wait()

        @pl.when(has_right)
        def _():
            pltpu.make_async_copy(
                edge_recv.at[m, slot, 1], edge_recv.at[m, slot, 1], edge_rsem.at[m, slot, 1]
            ).wait()

    lanes = lax.broadcasted_iota(jnp.int32, (8, 2 * chans), 1)

    def group_total(pair):
        total = jnp.broadcast_to(pair, (8, 2 * chans))
        step = 1
        while step < width:
            ahead = pltpu.roll(total, 2 * chans - step, 1)
            behind = pltpu.roll(total, step, 1)
            total = total + jnp.where((lanes // step) % 2 == 0, ahead, behind)
            step *= 2
        return total[0:1]

    def convolve(m, slot, layer, hidden, shift_row):
        stats = jnp.sum(st_recv[m, slot], axis=0)
        s1 = stats[:, 0:chans]
        s2 = stats[:, chans : 2 * chans]
        if shift_row is not None:
            s2 = s2 + 2.0 * shift_row * s1 + positions * (shift_row * shift_row)
            s1 = s1 + positions * shift_row
        total = group_total(jnp.concatenate([s1, s2], axis=1))
        mean = total[:, 0:chans] / count
        var = total[:, chans : 2 * chans] / count - mean * mean
        scale = lax.rsqrt(var + 1e-05) * gains[layer : layer + 1, :]
        offset = biases[layer : layer + 1, :] - mean * scale
        act = silu(hidden * scale + offset)
        edges = edge_recv[m, slot]
        if shift_row is not None:
            edges = edges + shift_row
        edges = silu(edges * scale + offset)
        before = jnp.where(has_left, edges[0], 0.0)
        after = jnp.where(has_right, edges[1], 0.0)
        place = lax.broadcasted_iota(jnp.int32, (frames, chans), 0)
        for f in range(rows_f):
            part = act[f * frames : (f + 1) * frames]
            prev = jnp.where(place == 0, before[f : f + 1], pltpu.roll(part, 1, 0))
            nxt = jnp.where(place == frames - 1, after[f : f + 1], pltpu.roll(part, frames - 1, 0))
            at = slice(f * frames, (f + 1) * frames)
            act3[at, 0:chans] = prev.astype(jnp.bfloat16)
            act3[at, chans : 2 * chans] = part.astype(jnp.bfloat16)
            act3[at, 2 * chans : 3 * chans] = nxt.astype(jnp.bfloat16)
        above, level, below = (
            jnp.dot(act3[span], w[layer, i], preferred_element_type=jnp.float32)
            for i, span in enumerate(
                (slice(0, rows - frames), slice(0, rows), slice(frames, rows))
            )
        )
        level = hidden + level
        inner = slice(frames, rows - frames)
        return jnp.concatenate(
            [
                level[:frames] + below[:frames],
                level[inner] + below[frames:] + above[: rows - 2 * frames],
                level[rows - frames :] + above[rows - 2 * frames :],
            ],
            axis=0,
        )

    def block_copy(m):
        return pltpu.make_async_remote_copy(
            src_ref=staged.at[m],
            dst_ref=xin.at[m],
            send_sem=blk_ssem.at[m],
            recv_sem=blk_rsem.at[m],
            device_id=(up, tm),
            device_id_type=MESH,
        )

    def finish(m, hidden):
        rounded = hidden.astype(jnp.bfloat16)
        staged[m] = rounded

        @pl.when(jnp.logical_not(last))
        def _():
            summarize(m, 2, rounded.astype(jnp.float32))
            publish(m, 2, 0, up, 0)
            block_copy(m).start()

    def enter(m):
        @pl.when(first)
        def _():
            await_stats(m, 0, 1)

        @pl.when(jnp.logical_not(first))
        def _():
            await_stats(m, 0, 0)
            pltpu.make_async_copy(xin.at[m], xin.at[m], blk_rsem.at[m]).wait()

        await_edges(m, 0)
        shift_row = temb[m : m + 1, :]
        hidden = xin[m].astype(jnp.float32) + shift_row
        hidden = convolve(m, 0, 0, hidden, shift_row)

        @pl.when(deep)
        def _():
            hmid[m] = hidden
            summarize(m, 1, hidden)
            publish(m, 1, 1, sec, 1)

        @pl.when(jnp.logical_not(deep))
        def _():
            finish(m, hidden)

    def leave(m):
        @pl.when(deep)
        def _():
            await_stats(m, 1, 1)
            await_edges(m, 1)
            finish(m, convolve(m, 1, 1, hmid[m], None))

    for copy in small[:4]:
        copy.wait()
    half = chans // 2
    slots = temb.shape[0]
    which = lax.broadcasted_iota(jnp.int32, (slots, half), 0)
    steps_f = jnp.zeros((slots, half), jnp.float32)
    for m in range(micros):
        steps_f = jnp.where(which == m, timestep[m].astype(jnp.float32), steps_f)

    @pl.when(first)
    def _():
        level = jnp.cos(math.pi / 2.0 * (steps_f / STEPS + 0.008) / 1.008) ** 2
        keep = jnp.sqrt(level)
        blur = jnp.sqrt(1.0 - level)
        for copy in small[4:]:
            copy.wait()
        for m in range(micros):
            noisy[m * rows_f : (m + 1) * rows_f, :] = (
                keep[m : m + 1, 0:1] * clean[m] + blur[m : m + 1, 0:1] * noise[m]
            )
        columns = jnp.transpose(noisy[...])
        for m in range(micros):
            for f in range(rows_f):
                at = m * rows_f + f
                xin[m, f * frames : (f + 1) * frames, :] = (
                    columns[:, at : at + 1] * lift[...]
                ).astype(jnp.bfloat16)
            summarize(m, 0, xin[m].astype(jnp.float32))

    order = lax.broadcasted_iota(jnp.int32, (slots, half), 1).astype(jnp.float32)
    angles = steps_f * jnp.exp(-math.log(10000.0) * order / half)
    temb[...] = jnp.dot(
        jnp.sin(angles).astype(jnp.bfloat16), proj[0:half, :], preferred_element_type=jnp.float32
    ) + jnp.dot(
        jnp.cos(angles).astype(jnp.bfloat16), proj[half:chans, :], preferred_element_type=jnp.float32
    )

    arrivals = n_time - 1 + n_time * jnp.where(last, 0, 1)
    pl.semaphore_wait(barrier, arrivals)

    @pl.when(first)
    def _():
        for m in range(micros):
            publish(m, 0, 0, sec, 1)

    load_w(0).wait()

    @pl.when(deep)
    def _():
        for layer in range(1, layers):
            load_w(layer).wait()

    enter(0)
    for m in range(1, micros):
        enter(m)
        leave(m - 1)
    leave(micros - 1)

    @pl.when(first)
    def _():
        for m in range(micros):
            drain(m, 0, 1)

    @pl.when(deep)
    def _():
        for m in range(micros):
            drain(m, 1, 1)

    @pl.when(jnp.logical_not(last))
    def _():
        for m in range(micros):
            drain(m, 2, 0)
            block_copy(m).wait_send()


def on_device(clean, noise, timestep, lift, norm_gain, norm_bias, conv_weight, time_proj):
    n_time = lax.axis_size("tm")
    n_section = lax.axis_size("section")
    micros, rows_f, frames = clean.shape
    chans = lift.shape[0]
    layers = norm_gain.shape[1]
    slots = -(-micros // 8) * 8
    rows = rows_f * frames
    dims = (n_time, n_section, micros, rows_f, frames, chans, layers)
    vmem = pl.BlockSpec(memory_space=pltpu.VMEM)
    hbm = pl.BlockSpec(memory_space=pl.ANY)
    dma = pltpu.SemaphoreType.DMA
    saved = pl.pallas_call(
        functools.partial(kernel, dims),
        out_shape=pltpu.VMEM((micros, rows, chans), jnp.bfloat16),
        in_specs=[hbm] * 8,
        out_specs=vmem,
        scratch_shapes=[
            pltpu.VMEM((layers, 3, 3 * chans, chans), jnp.bfloat16),
            pltpu.VMEM((micros, rows, chans), jnp.bfloat16),
            pltpu.VMEM((micros, rows, chans), jnp.float32),
            pltpu.VMEM((micros, rows_f, frames), jnp.float32),
            pltpu.VMEM((micros, rows_f, frames), jnp.float32),
            pltpu.VMEM((1, chans), jnp.float32),
            pltpu.VMEM((layers, chans), jnp.float32),
            pltpu.VMEM((layers, chans), jnp.float32),
            pltpu.VMEM((chans, chans), jnp.bfloat16),
            pltpu.VMEM((micros * rows_f, frames), jnp.float32),
            pltpu.VMEM((slots, chans), jnp.float32),
            pltpu.SMEM((micros,), jnp.int32),
            pltpu.VMEM((rows, 3 * chans), jnp.bfloat16),
            pltpu.VMEM((micros, 3, 1, 2 * chans), jnp.float32),
            pltpu.VMEM((micros, 2, n_time, 1, 2 * chans), jnp.float32),
            pltpu.VMEM((micros, 3, 2, rows_f, chans), jnp.float32),
            pltpu.VMEM((micros, 2, 2, rows_f, chans), jnp.float32),
            dma((micros, 3)),
            dma((micros, 2)),
            dma((micros, 3, 2)),
            dma((micros, 2, 2)),
            dma((micros,)),
            dma((micros,)),
            dma((layers,)),
            dma((7,)),
        ],
        compiler_params=pltpu.CompilerParams(
            collective_id=0, has_side_effects=True, vmem_limit_bytes=48 * 2**20
        ),
    )(
        *(
            pltpu.with_memory_space_constraint(x, pltpu.HBM)
            for x in (
                timestep,
                clean,
                noise,
                lift.reshape(1, chans),
                norm_gain,
                norm_bias,
                time_proj,
                conv_weight.reshape(layers, 3, 3 * chans, chans),
            )
        ),
    )
    return saved.reshape(1, micros, rows_f, frames, chans)


def solution(mesh):
    in_specs = (
        P(None, None, "tm"),
        P(None, None, "tm"),
        P(),
        P(),
        P("section", None, None),
        P("section", None, None),
        P("section", None, None, None, None, None),
        P("section", None, None),
    )
    out_specs = P("section", None, None, "tm", None)
    return jax.shard_map(
        on_device, mesh=mesh, in_specs=in_specs, out_specs=out_specs, check_vma=False
    )
```

```python
import functools
import math

import jax
import jax.numpy as jnp
from jax import lax
from jax.experimental import pallas as pl
from jax.experimental.pallas import tpu as pltpu
from jax.sharding import PartitionSpec as P

GROUPS = 32
STEPS = 1000
MESH = pl.DeviceIdType.MESH


def silu(z):
    half = 0.5 * z
    return half + half * jnp.tanh(half)


def kernel(
    dims,
    steps_in,
    clean_in,
    noise_in,
    lift_in,
    gains_in,
    biases_in,
    proj_in,
    weights,
    staged,
    w,
    xin,
    hmid,
    clean,
    noise,
    lift,
    gains,
    biases,
    proj,
    noisy,
    temb,
    timestep,
    act3,
    st_send,
    st_recv,
    edge_send,
    edge_recv,
    st_ssem,
    st_rsem,
    edge_ssem,
    edge_rsem,
    blk_ssem,
    blk_rsem,
    w_sem,
    in_sem,
):
    n_time, n_section, micros, rows_f, frames, chans, layers = dims
    rows = rows_f * frames
    positions = rows * n_time
    width = chans // GROUPS
    count = positions * width
    sec = lax.axis_index("section")
    tm = lax.axis_index("tm")
    deep = sec < n_section // 2
    first = sec == 0
    last = sec == n_section - 1
    has_left = tm > 0
    has_right = tm < n_time - 1
    up = jnp.minimum(sec + 1, n_section - 1)
    down = jnp.maximum(sec - 1, 0)
    short = n_time <= 8
    pieces = 1

    def load_w(layer):
        return pltpu.make_async_copy(weights.at[layer], w.at[layer], w_sem.at[layer])

    small = [
        pltpu.make_async_copy(src, dst, in_sem.at[k])
        for k, (src, dst) in enumerate(
            [
                (steps_in, timestep),
                (proj_in.at[0], proj),
                (gains_in.at[0], gains),
                (biases_in.at[0], biases),
                (clean_in, clean),
                (noise_in, noise),
                (lift_in, lift),
            ]
        )
    ]
    for copy in small[:4]:
        copy.start()

    @pl.when(first)
    def _():
        for copy in small[4:]:
            copy.start()

    barrier = pltpu.get_barrier_semaphore()

    def peers(section, begin):
        def one(r, carry):
            pl.semaphore_signal(
                barrier,
                inc=1,
                device_id=(section, lax.rem(tm + r, n_time)),
                device_id_type=MESH,
            )
            return carry

        lax.fori_loop(begin, n_time, one, 0, unroll=short)

    @pl.when(jnp.logical_not(first))
    def _():
        peers(down, 0)

    peers(sec, 1)

    load_w(0).start()

    @pl.when(deep)
    def _():
        for layer in range(1, layers):
            load_w(layer).start()

    def summarize(m, kind, value):
        st_send[m, kind, :, 0:chans] = jnp.sum(value, axis=0, keepdims=True)
        st_send[m, kind, :, chans : 2 * chans] = jnp.sum(value * value, axis=0, keepdims=True)
        for f in range(rows_f):
            edge_send[m, kind, 0, f : f + 1, :] = value[f * frames : f * frames + 1]
            edge_send[m, kind, 1, f : f + 1, :] = value[(f + 1) * frames - 1 : (f + 1) * frames]

    def edge_copy(m, kind, slot, side, section, peer):
        return pltpu.make_async_remote_copy(
            src_ref=edge_send.at[m, kind, side],
            dst_ref=edge_recv.at[m, slot, 1 - side],
            send_sem=edge_ssem.at[m, kind, side],
            recv_sem=edge_rsem.at[m, slot, 1 - side],
            device_id=(section, peer),
            device_id_type=MESH,
        )

    def publish(m, kind, slot, section, begin):
        def one(r, carry):
            pltpu.make_async_remote_copy(
                src_ref=st_send.at[m, kind],
                dst_ref=st_recv.at[m, slot, tm],
                send_sem=st_ssem.at[m, kind],
                recv_sem=st_rsem.at[m, slot],
                device_id=(section, lax.rem(tm + r, n_time)),
                device_id_type=MESH,
            ).start()
            return carry

        lax.fori_loop(begin, n_time, one, 0, unroll=short)
        if begin:
            st_recv[m, slot, tm] = st_send[m, kind]

        @pl.when(has_left)
        def _():
            edge_copy(m, kind, slot, 0, section, jnp.maximum(tm - 1, 0)).start()

        @pl.when(has_right)
        def _():
            edge_copy(m, kind, slot, 1, section, jnp.minimum(tm + 1, n_time - 1)).start()

    def drain(m, kind, begin):
        whole = st_recv.at[m, 0, pl.ds(0, n_time - begin)]
        pltpu.make_async_copy(whole, whole, st_ssem.at[m, kind]).wait()

        @pl.when(has_left)
        def _():
            pltpu.make_async_copy(
                edge_send.at[m, kind, 0], edge_send.at[m, kind, 0], edge_ssem.at[m, kind, 0]
            ).wait()

        @pl.when(has_right)
        def _():
            pltpu.make_async_copy(
                edge_send.at[m, kind, 1], edge_send.at[m, kind, 1], edge_ssem.at[m, kind, 1]
            ).wait()

    def await_stats(m, slot, begin):
        whole = st_recv.at[m, slot, pl.ds(0, n_time - begin)]
        pltpu.make_async_copy(whole, whole, st_rsem.at[m, slot]).wait()

    def await_edges(m, slot):
        @pl.when(has_left)
        def _():
            pltpu.make_async_copy(
                edge_recv.at[m, slot, 0], edge_recv.at[m, slot, 0], edge_rsem.at[m, slot, 0]
            ).wait()

        @pl.when(has_right)
        def _():
            pltpu.make_async_copy(
                edge_recv.at[m, slot, 1], edge_recv.at[m, slot, 1], edge_rsem.at[m, slot, 1]
            ).wait()

    lanes = lax.broadcasted_iota(jnp.int32, (8, 2 * chans), 1)

    def group_total(pair):
        total = jnp.broadcast_to(pair, (8, 2 * chans))
        step = 1
        while step < width:
            ahead = pltpu.roll(total, 2 * chans - step, 1)
            behind = pltpu.roll(total, step, 1)
            total = total + jnp.where((lanes // step) % 2 == 0, ahead, behind)
            step *= 2
        return total[0:1]

    def convolve(m, slot, layer, load, shift_row, parts):
        stats = jnp.sum(st_recv[m, slot], axis=0)
        s1 = stats[:, 0:chans]
        s2 = stats[:, chans : 2 * chans]
        if shift_row is not None:
            s2 = s2 + 2.0 * shift_row * s1 + positions * (shift_row * shift_row)
            s1 = s1 + positions * shift_row
        total = group_total(jnp.concatenate([s1, s2], axis=1))
        mean = total[:, 0:chans] / count
        var = total[:, chans : 2 * chans] / count - mean * mean
        scale = lax.rsqrt(var + 1e-05) * gains[layer : layer + 1, :]
        offset = biases[layer : layer + 1, :] - mean * scale
        edges = edge_recv[m, slot]
        if shift_row is not None:
            edges = edges + shift_row
        edges = silu(edges * scale + offset)
        before = jnp.where(has_left, edges[0], 0.0)
        after = jnp.where(has_right, edges[1], 0.0)
        place = lax.broadcasted_iota(jnp.int32, (frames, chans), 0)
        sums = [None] * rows_f

        def add(f, value):
            sums[f] = value if sums[f] is None else sums[f] + value

        for part in range(parts):
            low, high = part * rows_f // parts, (part + 1) * rows_f // parts
            hidden = load(part, slice(low * frames, high * frames))
            act = silu(hidden * scale + offset)
            for f in range(low, high):
                at = slice((f - low) * frames, (f - low + 1) * frames)
                add(f, hidden[at])
                row = act[at]
                prev = jnp.where(place == 0, before[f : f + 1], pltpu.roll(row, 1, 0))
                nxt = jnp.where(
                    place == frames - 1, after[f : f + 1], pltpu.roll(row, frames - 1, 0)
                )
                at = slice(f * frames, (f + 1) * frames)
                act3[at, 0:chans] = prev.astype(jnp.bfloat16)
                act3[at, chans : 2 * chans] = row.astype(jnp.bfloat16)
                act3[at, 2 * chans : 3 * chans] = nxt.astype(jnp.bfloat16)
            for i in range(3):
                used = [f for f in range(low, high) if 0 <= f - i + 1 < rows_f]
                if not used:
                    continue
                span = slice(used[0] * frames, (used[-1] + 1) * frames)
                product = jnp.dot(act3[span], w[layer, i], preferred_element_type=jnp.float32)
                for k, f in enumerate(used):
                    add(f - i + 1, product[k * frames : (k + 1) * frames])
        return jnp.concatenate(sums, axis=0)

    def piece(ref, m, part):
        height = rows_f // pieces * frames
        return ref.at[m, pl.ds(part * height, height)]

    def block_copy(m, part):
        return pltpu.make_async_remote_copy(
            src_ref=piece(staged, m, part),
            dst_ref=piece(xin, m, part),
            send_sem=blk_ssem.at[m, part],
            recv_sem=blk_rsem.at[m, part],
            device_id=(up, tm),
            device_id_type=MESH,
        )

    def finish(m, hidden):
        rounded = hidden.astype(jnp.bfloat16)
        staged[m] = rounded

        @pl.when(jnp.logical_not(last))
        def _():
            summarize(m, 2, rounded.astype(jnp.float32))
            publish(m, 2, 0, up, 0)
            for part in range(pieces):
                block_copy(m, part).start()

    def enter(m):
        @pl.when(first)
        def _():
            await_stats(m, 0, 1)

        @pl.when(jnp.logical_not(first))
        def _():
            await_stats(m, 0, 0)

        await_edges(m, 0)
        shift_row = temb[m : m + 1, :]

        def load(part, span):
            @pl.when(jnp.logical_not(first))
            def _():
                landed = piece(xin, m, part)
                pltpu.make_async_copy(landed, landed, blk_rsem.at[m, part]).wait()

            return xin[m, span, :].astype(jnp.float32) + shift_row

        hidden = convolve(m, 0, 0, load, shift_row, pieces)

        @pl.when(deep)
        def _():
            hmid[m] = hidden
            summarize(m, 1, hidden)
            publish(m, 1, 1, sec, 1)

        @pl.when(jnp.logical_not(deep))
        def _():
            finish(m, hidden)

    def leave(m):
        @pl.when(deep)
        def _():
            await_stats(m, 1, 1)
            await_edges(m, 1)
            finish(m, convolve(m, 1, 1, lambda part, span: hmid[m, span, :], None, 1))

    for copy in small[:4]:
        copy.wait()
    half = chans // 2
    slots = temb.shape[0]
    which = lax.broadcasted_iota(jnp.int32, (slots, half), 0)
    steps_f = jnp.zeros((slots, half), jnp.float32)
    for m in range(micros):
        steps_f = jnp.where(which == m, timestep[m].astype(jnp.float32), steps_f)

    @pl.when(first)
    def _():
        level = jnp.cos(math.pi / 2.0 * (steps_f / STEPS + 0.008) / 1.008) ** 2
        keep = jnp.sqrt(level)
        blur = jnp.sqrt(1.0 - level)
        for copy in small[4:]:
            copy.wait()
        for m in range(micros):
            noisy[m * rows_f : (m + 1) * rows_f, :] = (
                keep[m : m + 1, 0:1] * clean[m] + blur[m : m + 1, 0:1] * noise[m]
            )
        columns = jnp.transpose(noisy[...])
        for m in range(micros):
            for f in range(rows_f):
                at = m * rows_f + f
                xin[m, f * frames : (f + 1) * frames, :] = (
                    columns[:, at : at + 1] * lift[...]
                ).astype(jnp.bfloat16)
            summarize(m, 0, xin[m].astype(jnp.float32))

    order = lax.broadcasted_iota(jnp.int32, (slots, half), 1).astype(jnp.float32)
    angles = steps_f * jnp.exp(-math.log(10000.0) * order / half)
    temb[...] = jnp.dot(
        jnp.sin(angles).astype(jnp.bfloat16), proj[0:half, :], preferred_element_type=jnp.float32
    ) + jnp.dot(
        jnp.cos(angles).astype(jnp.bfloat16), proj[half:chans, :], preferred_element_type=jnp.float32
    )

    arrivals = n_time - 1 + n_time * jnp.where(last, 0, 1)
    pl.semaphore_wait(barrier, arrivals)

    @pl.when(first)
    def _():
        for m in range(micros):
            publish(m, 0, 0, sec, 1)

    load_w(0).wait()

    @pl.when(deep)
    def _():
        for layer in range(1, layers):
            load_w(layer).wait()

    enter(0)
    for m in range(1, micros):
        enter(m)
        leave(m - 1)
    leave(micros - 1)

    @pl.when(first)
    def _():
        for m in range(micros):
            drain(m, 0, 1)

    @pl.when(deep)
    def _():
        for m in range(micros):
            drain(m, 1, 1)

    @pl.when(jnp.logical_not(last))
    def _():
        for m in range(micros):
            drain(m, 2, 0)
            for part in range(pieces):
                block_copy(m, part).wait_send()


def on_device(clean, noise, timestep, lift, norm_gain, norm_bias, conv_weight, time_proj):
    n_time = lax.axis_size("tm")
    n_section = lax.axis_size("section")
    micros, rows_f, frames = clean.shape
    chans = lift.shape[0]
    layers = norm_gain.shape[1]
    slots = -(-micros // 8) * 8
    rows = rows_f * frames
    dims = (n_time, n_section, micros, rows_f, frames, chans, layers)
    vmem = pl.BlockSpec(memory_space=pltpu.VMEM)
    hbm = pl.BlockSpec(memory_space=pl.ANY)
    dma = pltpu.SemaphoreType.DMA
    saved = pl.pallas_call(
        functools.partial(kernel, dims),
        out_shape=pltpu.VMEM((micros, rows, chans), jnp.bfloat16),
        in_specs=[hbm] * 8,
        out_specs=vmem,
        scratch_shapes=[
            pltpu.VMEM((layers, 3, 3 * chans, chans), jnp.bfloat16),
            pltpu.VMEM((micros, rows, chans), jnp.bfloat16),
            pltpu.VMEM((micros, rows, chans), jnp.float32),
            pltpu.VMEM((micros, rows_f, frames), jnp.float32),
            pltpu.VMEM((micros, rows_f, frames), jnp.float32),
            pltpu.VMEM((1, chans), jnp.float32),
            pltpu.VMEM((layers, chans), jnp.float32),
            pltpu.VMEM((layers, chans), jnp.float32),
            pltpu.VMEM((chans, chans), jnp.bfloat16),
            pltpu.VMEM((micros * rows_f, frames), jnp.float32),
            pltpu.VMEM((slots, chans), jnp.float32),
            pltpu.SMEM((micros,), jnp.int32),
            pltpu.VMEM((rows, 3 * chans), jnp.bfloat16),
            pltpu.VMEM((micros, 3, 1, 2 * chans), jnp.float32),
            pltpu.VMEM((micros, 2, n_time, 1, 2 * chans), jnp.float32),
            pltpu.VMEM((micros, 3, 2, rows_f, chans), jnp.float32),
            pltpu.VMEM((micros, 2, 2, rows_f, chans), jnp.float32),
            dma((micros, 3)),
            dma((micros, 2)),
            dma((micros, 3, 2)),
            dma((micros, 2, 2)),
            dma((micros, 2)),
            dma((micros, 2)),
            dma((layers,)),
            dma((7,)),
        ],
        compiler_params=pltpu.CompilerParams(
            collective_id=0, has_side_effects=True, vmem_limit_bytes=48 * 2**20
        ),
    )(
        *(
            pltpu.with_memory_space_constraint(x, pltpu.HBM)
            for x in (
                timestep,
                clean,
                noise,
                lift.reshape(1, chans),
                norm_gain,
                norm_bias,
                time_proj,
                conv_weight.reshape(layers, 3, 3 * chans, chans),
            )
        ),
    )
    return saved.reshape(1, micros, rows_f, frames, chans)


def solution(mesh):
    in_specs = (
        P(None, None, "tm"),
        P(None, None, "tm"),
        P(),
        P(),
        P("section", None, None),
        P("section", None, None),
        P("section", None, None, None, None, None),
        P("section", None, None),
    )
    out_specs = P("section", None, None, "tm", None)
    return jax.shard_map(
        on_device, mesh=mesh, in_specs=in_specs, out_specs=out_specs, check_vma=False
    )
```
